32 devices in a mesh: ctx: 8 (over y, x, core), head: 4 (over z).
Axes of the slice: x: 2, y: 2, z: 4, core: 2. Of those that a mesh axis runs over, the one named last changes fastest.
Arguments:
- inputs: bfloat16 [2048, 4096], P('ctx', 'head'), may hold values from -6 to 6
- log_decay: float32 [64, 2048], P('head', 'ctx'), may hold values from -1 to 0
- in_b: bfloat16 [2048, 512], P('ctx', 'head'), may hold values from -0.20996094 to 0.20996094
- in_c: bfloat16 [2048, 512], P('ctx', 'head'), may hold values from -0.20996094 to 0.20996094
- seg_ids: int32 [2048], P('ctx'), may hold values from 0 to 5, never falling along the last dimension, each value on 1 to 1024 neighbouring positions
- skip_gain: float32 [64], P('head'), may hold values from 0.1 to 1.9
- grad_out: bfloat16 [2048, 4096], P('ctx', 'head'), may hold values from -0.119628906 to 0.119628906
Outputs:
- ssd_out: bfloat16 [2048, 4096], P('ctx', 'head')
- grad_x: bfloat16 [2048, 4096], P('ctx', 'head')
- grad_b: bfloat16 [2048, 512], P('ctx', 'head')
- grad_c: bfloat16 [2048, 512], P('ctx', 'head')
The draws below stay inside these ranges and needn't reach their ends.
All inputs are finite; a program needn't handle non-finite values.
Results may differ from the reference program's by a relative error of at most 0.0017.
Values may be sent and summed in bfloat16 or wider, within the bound.
A program may use at most 192 MiB of HBM per device.

```python
import math
import jax
import jax.numpy as jnp
import numpy as np
from jax import lax

HEAD_SIZE = 64
STATE = 256
BLOCK = 256
HEADS = 64
GROUPS = 2
SEQUENCE_TOKENS = 2048


def draw_log_decay(key, part):
    random_key_variety, random_key_quick, random_key_gradual, random_key_wobble, random_key_spike, random_key_missing = jax.random.split(key, 6)
    fast_share = 0.5
    fast_heads = jax.random.bernoulli(random_key_variety, fast_share, (HEADS, 1))
    fast_rate = jnp.exp(jax.random.uniform(random_key_quick, (HEADS, 1), jnp.float32, math.log(1.0 / 50.0), math.log(1.0 / 30.0)))
    slow_rate = math.log(2.5) / SEQUENCE_TOKENS * jax.random.uniform(random_key_gradual, (HEADS, 1), jnp.float32, 0.5, 1.0)
    baseline_rate = jnp.where(fast_heads, fast_rate, slow_rate)
    random_wobble = jnp.exp(jax.random.uniform(random_key_wobble, (HEADS, SEQUENCE_TOKENS), jnp.float32, math.log(0.5), math.log(2.0)))
    spike_locations = jax.random.randint(random_key_spike, (2,), 0, SEQUENCE_TOKENS)
    token_places = jnp.arange(SEQUENCE_TOKENS)
    spike_mask = jnp.any(token_places[None, :] == spike_locations[:, None], axis=0)
    missing_fraction = jax.random.uniform(random_key_missing, (HEADS, SEQUENCE_TOKENS), jnp.float32, 0.2, 0.5)
    spike_decrease = jnp.where(spike_mask[None, :], jnp.log(1.0 - missing_fraction), 0.0)
    return (spike_decrease - baseline_rate * random_wobble).astype(jnp.float32)


def levels(rng, shape, shards, least, high):
    factor_of = 1.0
    for axis_at, blocks in shards:
        draws = jax.random.uniform(jax.random.fold_in(jax.random.fold_in(rng, 6), axis_at), (blocks,), jnp.float32, least / len(shards), high / len(shards))
        factor_of = factor_of * jnp.repeat(jnp.exp(draws), shape[axis_at] // blocks).reshape((-1,) + (1,) * (len(shape) - 1 - axis_at))
    return factor_of


def split_up(amount, total, bound, slope):
    weights = [(1 << 20) // math.isqrt(rank ** slope) + 1 for rank in range(2, amount + 1)]
    spare, counts = total - bound - (amount - 1), [1] * (amount - 1)
    while spare > 0:
        candidates = [i for i in range(amount - 1) if counts[i] < bound]
        whole, budget = sum([weights[i] for i in candidates]), spare
        for i in candidates:
            extra = min(bound - counts[i], max(1, budget * weights[i] // whole), spare)
            counts[i] = counts[i] + extra
            spare = spare - extra
    return np.array([bound] + counts)


def uneven_parts(key, amount, total, bound, skew):
    if amount == 2:
        one = jax.random.randint(key, (), max(1, total - bound), min(bound, total - 1) + 1)
        return jnp.stack([one, total - one])
    tallies = jnp.asarray(split_up(amount, total, bound, skew), jnp.int32)
    couples = (amount - 1) // 2
    giver, receiver = tallies[1:1 + 2 * couples:2], tallies[2:2 + 2 * couples:2]
    slack = jnp.minimum(giver - 1, bound - receiver)
    shifted = jax.random.randint(jax.random.fold_in(key, 1), (couples,), 0, 1 << 20) % (slack + 1)
    tallies = tallies.at[1:1 + 2 * couples:2].set(giver - shifted).at[2:2 + 2 * couples:2].set(receiver + shifted)
    return tallies[jax.random.permutation(jax.random.fold_in(key, 2), amount)]


def gaussian(key, extent, deviation, bound, cuts=(), kind=jnp.bfloat16):
    entries = jax.random.normal(key, extent, jnp.float32) * deviation
    if len(cuts) > 0:
        entries = levels(key, extent, cuts, -0.22, 0.18) * entries
    return jnp.clip(entries, min=-bound, max=bound).astype(kind)


def setup_inputs(seed: int = 0) -> dict:
    key_of = jax.random.split(jax.random.key(seed), 8)
    return {
        "inputs": gaussian(key_of[0], (SEQUENCE_TOKENS, HEADS * HEAD_SIZE), 1.0, 6.0, ((0, 8), (1, 4))),
        "log_decay": draw_log_decay(jax.random.fold_in(key_of[7], 71), 0),
        "in_b": gaussian(key_of[2], (SEQUENCE_TOKENS, GROUPS * STATE), 0.035, 0.20996094, ((0, 8), (1, 4))),
        "in_c": gaussian(key_of[3], (SEQUENCE_TOKENS, GROUPS * STATE), 0.035, 0.20996094, ((0, 8), (1, 4))),
        "seg_ids": jnp.searchsorted(jnp.cumsum(uneven_parts(key_of[4], 6, SEQUENCE_TOKENS, SEQUENCE_TOKENS // 2, 0)), jnp.arange(SEQUENCE_TOKENS), side="right").astype(jnp.int32),
        "skip_gain": jnp.clip(1.0 + 0.18 * jax.random.normal(key_of[5], (HEADS,), jnp.float32), 0.1, 1.9),
        "grad_out": gaussian(key_of[6], (SEQUENCE_TOKENS, HEADS * HEAD_SIZE), 0.02, 0.119628906, ((0, 8), (1, 4))),
    }


highest = lax.Precision.HIGHEST


def block_tables(decay_rows, seg_block, prev_seg):
    cum_decay = jnp.cumsum(decay_rows, axis=-1)
    total_decay = cum_decay[..., -1]
    last_seg = seg_block[-1]
    row_index = jnp.arange(seg_block.shape[0])
    keep_mask = (row_index[:, None] >= row_index[None, :]) & (seg_block[:, None] == seg_block[None, :])
    decay_table = jnp.exp(jnp.where(keep_mask, cum_decay[..., :, None] - cum_decay[..., None, :], -jnp.inf))
    start_weight = jnp.exp(cum_decay) * (seg_block == prev_seg).astype(cum_decay.dtype)
    end_weight = jnp.exp(total_decay[..., None] - cum_decay) * (seg_block == last_seg).astype(cum_decay.dtype)
    carry_gain = jnp.exp(total_decay) * (last_seg == prev_seg).astype(cum_decay.dtype)
    return decay_table, start_weight, end_weight, carry_gain, last_seg


def block_mix(decay_table, b_float, c_float):
    score = jnp.einsum('ign,jgn->gij', c_float, b_float, precision=highest)
    return (decay_table * score[:, None]).astype(jnp.bfloat16).astype(jnp.float32)


def reference(inputs, log_decay, in_b, in_c, seg_ids, skip_gain, grad_out):
    per_group = HEADS // GROUPS
    block_total = SEQUENCE_TOKENS // BLOCK
    input_blocks = inputs.reshape(block_total, BLOCK, GROUPS, per_group, HEAD_SIZE)
    grad_blocks = grad_out.reshape(block_total, BLOCK, GROUPS, per_group, HEAD_SIZE)
    decay_blocks = log_decay.reshape(GROUPS, per_group, block_total, BLOCK).transpose(2, 0, 1, 3)
    seg_blocks = seg_ids.reshape(block_total, BLOCK)
    b_blocks = in_b.reshape(block_total, BLOCK, GROUPS, STATE)
    c_blocks = in_c.reshape(block_total, BLOCK, GROUPS, STATE)
    gains = skip_gain.reshape(GROUPS, per_group)

    def forward_block(carried, block):
        state_now, prev_seg = carried
        x_block, decay_rows, seg_block, b_block, c_block = block
        decay_table, start_weight, end_weight, carry_gain, last_seg = block_tables(decay_rows, seg_block, prev_seg)
        b_float = b_block.astype(jnp.float32)
        c_float = c_block.astype(jnp.float32)
        x_float = x_block.astype(jnp.float32)
        mixed = block_mix(decay_table, b_float, c_float)
        inner_term = jnp.einsum('ghij,jghp->ighp', mixed, x_float, precision=highest)
        outer_term = jnp.einsum('ign,ghpn->ighp', c_float, state_now, precision=highest)
        outer_term = outer_term * jnp.transpose(start_weight, (2, 0, 1))[..., None]
        weighted = x_float * jnp.transpose(end_weight, (2, 0, 1))[..., None]
        fresh_state = jnp.einsum('jghp,jgn->ghpn', weighted, b_float, precision=highest)
        next_state = carry_gain[..., None, None] * state_now + fresh_state
        return (next_state, last_seg), (inner_term + outer_term, state_now, prev_seg)

    start_state = jnp.zeros((GROUPS, per_group, HEAD_SIZE, STATE), jnp.float32)
    start_seg = jnp.array(-1, seg_ids.dtype)
    _, (scan_terms, entering, prev_segs) = lax.scan(
        forward_block, (start_state, start_seg), (input_blocks, decay_blocks, seg_blocks, b_blocks, c_blocks))
    x_all = input_blocks.astype(jnp.float32)
    ssd_out = (scan_terms + gains[None, None, :, :, None] * x_all).astype(jnp.bfloat16)
    ssd_out = ssd_out.reshape(SEQUENCE_TOKENS, HEADS * HEAD_SIZE)

    def backward_block(adjoint, block):
        x_block, decay_rows, seg_block, b_block, c_block, grad_block, state_now, prev_seg = block
        decay_table, start_weight, end_weight, carry_gain, last_seg = block_tables(decay_rows, seg_block, prev_seg)
        b_float = b_block.astype(jnp.float32)
        c_float = c_block.astype(jnp.float32)
        x_float = x_block.astype(jnp.float32)
        grad_float = grad_block.astype(jnp.float32)
        mixed = block_mix(decay_table, b_float, c_float)
        end_t = jnp.transpose(end_weight, (2, 0, 1))[..., None]
        start_t = jnp.transpose(start_weight, (2, 0, 1))[..., None]
        grad_inputs = jnp.einsum('ghij,ighp->jghp', mixed, grad_float, precision=highest)
        grad_inputs = grad_inputs + jnp.einsum('jgn,ghpn->jghp', b_float, adjoint, precision=highest) * end_t
        grad_mix = jnp.einsum('ighp,jghp->ghij', grad_float, x_float, precision=highest)
        dscore = jnp.sum(grad_mix * decay_table, axis=1)
        grad_bmap = jnp.einsum('gij,ign->jgn', dscore, c_float, precision=highest)
        grad_bmap = grad_bmap + jnp.einsum('jghp,ghpn->jgn', x_float * end_t, adjoint, precision=highest)
        grad_cmap = jnp.einsum('gij,jgn->ign', dscore, b_float, precision=highest)
        grad_start = grad_float * start_t
        grad_cmap = grad_cmap + jnp.einsum('ighp,ghpn->ign', grad_start, state_now, precision=highest)
        back_state = jnp.einsum('ighp,ign->ghpn', grad_start, c_float, precision=highest)
        next_adjoint = back_state + carry_gain[..., None, None] * adjoint
        return next_adjoint, (grad_inputs, grad_bmap, grad_cmap)

    _, (grad_terms, grad_bmaps, grad_cmaps) = lax.scan(
        backward_block, jnp.zeros((GROUPS, per_group, HEAD_SIZE, STATE), jnp.float32),
        (input_blocks, decay_blocks, seg_blocks, b_blocks, c_blocks, grad_blocks, entering, prev_segs),
        reverse=True)
    grad_all = grad_blocks.astype(jnp.float32)
    grad_x = (grad_terms + gains[None, None, :, :, None] * grad_all).astype(jnp.bfloat16)
    grad_x = grad_x.reshape(SEQUENCE_TOKENS, HEADS * HEAD_SIZE)
    grad_b = grad_bmaps.astype(jnp.bfloat16).reshape(SEQUENCE_TOKENS, GROUPS * STATE)
    grad_c = grad_cmaps.astype(jnp.bfloat16).reshape(SEQUENCE_TOKENS, GROUPS * STATE)
    return ssd_out, grad_x, grad_b, grad_c
```

```python
import functools

import jax
import jax.numpy as jnp
from jax import lax
from jax.experimental import pallas as pl
from jax.experimental.pallas import tpu as pltpu
from jax.sharding import PartitionSpec as P

MESH = pl.DeviceIdType.MESH
BF = jnp.bfloat16
F32 = jnp.float32
NT = (((1,), (1,)), ((), ()))
NN = (((1,), (0,)), ((), ()))
TN = (((0,), (0,)), ((), ()))


def mm(a, b, dims=NN):
    return lax.dot_general(a, b, dims, preferred_element_type=F32)


def split(v):
    hi = v.astype(BF)
    return hi, (v - hi.astype(F32)).astype(BF)


def kernel(
    peers, x_ref, ld_ref, b_ref, c_ref, seg_ref, skip_ref, d_ref,
    ssd_ref, gx_ref, gb_ref, gc_ref,
    bc, info, acum_s, acx, we_s, ws_s, wxh, wxl, wdh, wdl, bias, score_s, dsc,
    ssd_acc, gx_acc, fg, full, half, tbuf, slots, st, gacc, grecv,
    bc_send, bc_recv, i_send, i_recv, d_send, d_recv, t_send, t_recv, s_send, s_recv, g_send, g_recv,
):
    tokens, width = x_ref.shape
    heads = ld_ref.shape[0]
    head = width // heads
    hw = width // 2
    pairs = width // 128
    chips = peers // 2
    me = lax.axis_index("ctx")
    hd = lax.axis_index("head")
    side = hd % 2
    mate = hd + 1 - 2 * side
    core = me % 2
    chip = me // 2
    sib = me + 1 - 2 * core

    barrier = pltpu.get_barrier_semaphore()
    for off in range(1, peers):
        pl.semaphore_signal(barrier, inc=1, device_id={"ctx": (me + off) % peers}, device_id_type=MESH)
    pl.semaphore_signal(barrier, inc=1, device_id={"head": mate}, device_id_type=MESH)

    low = lax.broadcasted_iota(jnp.int32, (1, 128), 1) < head
    rows = lax.broadcasted_iota(jnp.int32, (tokens, tokens), 0)
    cols = lax.broadcasted_iota(jnp.int32, (tokens, tokens), 1)
    ones = jnp.where(rows <= cols, 1.0, 0.0).astype(BF)
    ld = ld_ref[...]
    l0 = ld.astype(BF)
    r1 = ld - l0.astype(F32)
    l1 = r1.astype(BF)
    l2 = (r1 - l1.astype(F32)).astype(BF)
    acum = mm(l0, ones) + mm(l1, ones) + mm(l2, ones)
    acum_s[...] = acum
    acum_t = jnp.concatenate([acum, jnp.zeros((128 - heads, tokens), F32)], axis=0).T
    for p in range(pairs):
        acx[:, p * 128 : (p + 1) * 128] = jnp.where(
            low, acum_t[:, 2 * p : 2 * p + 1], acum_t[:, 2 * p + 1 : 2 * p + 2]
        )
    seg_row = seg_ref[...].astype(F32)
    seg_col = jnp.broadcast_to(seg_row, (128, tokens)).T
    last = jnp.broadcast_to(seg_row[:, tokens - 1 : tokens], (1, hw))
    info[me, 0:1, :] = acx[tokens - 1 : tokens, 0:hw]
    info[me, 1:2, :] = acx[tokens - 1 : tokens, hw:width]
    info[me, 2:3, :] = last
    info[me, 3:4, :] = last

    pl.semaphore_wait(barrier, peers)

    bc_copies = []
    for k, ref in enumerate((b_ref, c_ref)):
        copy = pltpu.make_async_remote_copy(
            src_ref=ref, dst_ref=bc.at[k, side], send_sem=bc_send.at[k], recv_sem=bc_recv.at[k],
            device_id={"head": mate}, device_id_type=MESH)
        copy.start()
        bc_copies.append(copy)
    i_copies = []
    for off in range(1, peers):
        copy = pltpu.make_async_remote_copy(
            src_ref=info.at[me], dst_ref=info.at[me], send_sem=i_send.at[off - 1], recv_sem=i_recv.at[off - 1],
            device_id={"ctx": (me + off) % peers}, device_id_type=MESH)
        copy.start()
        i_copies.append(copy)
    bc[0, side] = b_ref[...]
    bc[1, side] = c_ref[...]

    bias[...] = jnp.where(
        (rows >= cols) & (jnp.concatenate([seg_col] * (tokens // 128), axis=1) == seg_row), 0.0, -1e30
    )
    end_mask = jnp.where(seg_col == last[:, 0:128], 1.0, 0.0)
    for p in range(pairs):
        s = slice(p * 128, (p + 1) * 128)
        a = acx[:, s]
        we = jnp.exp(a[tokens - 1 : tokens, :] - a) * end_mask
        we_s[:, s] = we
        hi, lo = split(x_ref[:, s].astype(F32) * we)
        wxh[:, s] = hi
        wxl[:, s] = lo

    for off in range(1, peers):
        src = (me + peers - off) % peers
        pltpu.make_async_remote_copy(
            src_ref=info.at[src], dst_ref=info.at[src], send_sem=i_send.at[off - 1], recv_sem=i_recv.at[off - 1],
            device_id={"ctx": (me + off) % peers}, device_id_type=MESH).wait_recv()

    def seg_of(i):
        return info[(i + peers) % peers, 2:3, :]

    def prev_seg(i):
        return jnp.where(i == 0, -1.0, seg_of(i - 1))

    start_mask = jnp.where(seg_col == prev_seg(me)[:, 0:128], 1.0, 0.0)
    for p in range(pairs):
        s = slice(p * 128, (p + 1) * 128)
        ws = jnp.exp(acx[:, s]) * start_mask
        ws_s[:, s] = ws
        hi, lo = split(d_ref[:, s].astype(F32) * ws)
        wdh[:, s] = hi
        wdl[:, s] = lo

    for copy in bc_copies:
        copy.wait_recv()
    b_full = jnp.concatenate([bc[0, 0], bc[0, 1]], axis=1)
    c_full = jnp.concatenate([bc[1, 0], bc[1, 1]], axis=1)
    b_t = b_full.T
    c_t = c_full.T
    for k in range(2):
        s = slice(k * hw, (k + 1) * hw)
        fg[0, k] = mm(b_t, wxh[:, s]) + mm(b_t, wxl[:, s])
        fg[1, k] = mm(c_t, wdh[:, s]) + mm(c_t, wdl[:, s])

    half_copy = pltpu.make_async_remote_copy(
        src_ref=fg.at[1 - core, 1 - core], dst_ref=half, send_sem=d_send.at[0], recv_sem=d_recv.at[0],
        device_id={"ctx": sib}, device_id_type=MESH)
    half_copy.start()
    full_copy = pltpu.make_async_remote_copy(
        src_ref=fg.at[core], dst_ref=full, send_sem=d_send.at[1], recv_sem=d_recv.at[1],
        device_id={"ctx": sib}, device_id_type=MESH)
    full_copy.start()

    def carry(i, k):
        return jnp.exp(info[i, pl.ds(k, 1), :]) * jnp.where(seg_of(i) == prev_seg(i), 1.0, 0.0)

    half_copy.wait_recv()
    tbuf[core] = half[...] + carry(sib, core) * fg[core, core]
    full_copy.wait_recv()
    tbuf[1 - core] = fg[1 - core, core] + carry(me, core) * full[core]
    t_copies = []
    for off in range(1, chips):
        copy = pltpu.make_async_remote_copy(
            src_ref=tbuf.at[(chip + off) // chips], dst_ref=slots.at[off - 1],
            send_sem=t_send.at[off - 1], recv_sem=t_recv.at[off - 1],
            device_id={"ctx": ((chip + off) % chips) * 2 + core}, device_id_type=MESH)
        copy.start()
        t_copies.append(copy)

    score_s[...] = mm(c_full, b_full, NT)
    dsc[...] = jnp.zeros_like(dsc)

    def pair_step(p, carried):
        s = pl.ds(pl.multiple_of(p * 128, 128), 128)
        x = x_ref[:, s]
        d = d_ref[:, s]
        gain = jnp.where(low, skip_ref[2 * p], skip_ref[2 * p + 1])
        out = gain * x.astype(F32)
        gx = gain * d.astype(F32)
        zero = jnp.zeros_like(x)
        total = dsc[...]
        for k in range(2):
            mine = low if k == 0 else jnp.logical_not(low)
            xm = jnp.where(mine, x, zero)
            dm = jnp.where(mine, d, zero)
            a_col = acx[:, s][:, k * head : k * head + 1]
            a_row = acum_s[pl.ds(2 * p + k, 1), :]
            table = jnp.exp((a_col - a_row) + bias[...])
            mixed = (table * score_s[...]).astype(BF)
            out = out + mm(mixed, xm)
            gx = gx + mm(mixed, dm, TN)
            total = total + mm(dm, x, NT) * table
        dsc[...] = total
        ssd_acc[:, s] = out
        gx_acc[:, s] = gx
        return carried

    lax.fori_loop(0, pairs, pair_step, 0)

    ds_hi, ds_lo = split(dsc[...])
    gb = mm(ds_hi, c_full, TN) + mm(ds_lo, c_full, TN)
    gc = mm(ds_hi, b_full) + mm(ds_lo, b_full)

    st[core, 0] = jnp.zeros(st.shape[2:], F32)
    st[core, 1] = jnp.zeros(st.shape[2:], F32)
    for off in range(1, chips):
        src = (chip + chips - off) % chips
        later = 1 - (chip + chips - off) // chips
        first = jnp.minimum(src, chip)
        final = jnp.maximum(src, chip)
        total = jnp.zeros((1, hw), F32)
        for i in range(peers):
            within = (i >= 2 * first + 2) & (i < 2 * final)
            total = total + jnp.where(within, info[i, pl.ds(core, 1), :], 0.0)
        weight = jnp.exp(total) * jnp.where(seg_of(2 * first + 1) == seg_of(2 * final - 1), 1.0, 0.0)
        pltpu.make_async_remote_copy(
            src_ref=tbuf.at[0], dst_ref=slots.at[off - 1],
            send_sem=t_send.at[off - 1], recv_sem=t_recv.at[off - 1],
            device_id={"ctx": ((chip + off) % chips) * 2 + core}, device_id_type=MESH).wait_recv()
        st[core, later] = st[core, later] + weight * slots[off - 1]
    s_copy = pltpu.make_async_remote_copy(
        src_ref=st.at[core], dst_ref=st.at[core], send_sem=s_send, recv_sem=s_recv,
        device_id={"ctx": sib}, device_id_type=MESH)
    s_copy.start()
    s_copy.wait_send()
    pltpu.make_async_remote_copy(
        src_ref=st.at[1 - core], dst_ref=st.at[1 - core], send_sem=s_send, recv_sem=s_recv,
        device_id={"ctx": sib}, device_id_type=MESH).wait_recv()
    for k in range(2):
        st[k, 1 - core] = carry(sib, k) * st[k, 1 - core] + full[k]

    for k in range(2):
        s = slice(k * hw, (k + 1) * hw)
        s_hi, s_lo = split(st[k, 0])
        a_hi, a_lo = split(st[k, 1])
        gb = gb + mm(wxh[:, s], a_hi, NT) + mm(wxl[:, s], a_hi, NT) + mm(wxh[:, s], a_lo, NT)
        gc = gc + mm(wdh[:, s], s_hi, NT) + mm(wdl[:, s], s_hi, NT) + mm(wdh[:, s], s_lo, NT)
    n = gb.shape[1] // 2
    for k in range(2):
        gacc[k, 0] = gb[:, k * n : (k + 1) * n]
        gacc[k, 1] = gc[:, k * n : (k + 1) * n]
    g_copy = pltpu.make_async_remote_copy(
        src_ref=gacc.at[1 - side], dst_ref=grecv, send_sem=g_send, recv_sem=g_recv,
        device_id={"head": mate}, device_id_type=MESH)
    g_copy.start()

    for k in range(2):
        s = slice(k * hw, (k + 1) * hw)
        s_hi, s_lo = split(st[k, 0])
        a_hi, a_lo = split(st[k, 1])
        ssd_ref[:, s] = (ssd_acc[:, s] + ws_s[:, s] * (mm(c_full, s_hi) + mm(c_full, s_lo))).astype(BF)
        gx_ref[:, s] = (gx_acc[:, s] + we_s[:, s] * (mm(b_full, a_hi) + mm(b_full, a_lo))).astype(BF)

    g_copy.wait_recv()
    gb_ref[...] = (gacc[side, 0] + grecv[0]).astype(BF)
    gc_ref[...] = (gacc[side, 1] + grecv[1]).astype(BF)

    for copy in bc_copies + i_copies + [half_copy, full_copy] + t_copies + [g_copy]:
        copy.wait_send()


def per_device(peers, inputs, log_decay, in_b, in_c, seg_ids, skip_gain, grad_out):
    tokens, width = inputs.shape
    heads = log_decay.shape[0]
    cols = in_b.shape[1]
    n = 2 * cols
    hw = width // 2
    chips = peers // 2
    vm = pl.BlockSpec(memory_space=pltpu.VMEM)
    dma = pltpu.SemaphoreType.DMA
    return pl.pallas_call(
        functools.partial(kernel, peers),
        out_shape=(
            jax.ShapeDtypeStruct((tokens, width), BF),
            jax.ShapeDtypeStruct((tokens, width), BF),
            jax.ShapeDtypeStruct((tokens, cols), BF),
            jax.ShapeDtypeStruct((tokens, cols), BF),
        ),
        in_specs=[vm, vm, vm, vm, vm, pl.BlockSpec(memory_space=pltpu.SMEM), vm],
        out_specs=(vm, vm, vm, vm),
        scratch_shapes=[
            pltpu.VMEM((2, 2, tokens, cols), BF),
            pltpu.VMEM((peers, 4, hw), F32),
            pltpu.VMEM((heads, tokens), F32),
            pltpu.VMEM((tokens, width), F32),
            pltpu.VMEM((tokens, width), F32),
            pltpu.VMEM((tokens, width), F32),
            pltpu.VMEM((tokens, width), BF),
            pltpu.VMEM((tokens, width), BF),
            pltpu.VMEM((tokens, width), BF),
            pltpu.VMEM((tokens, width), BF),
            pltpu.VMEM((tokens, tokens), F32),
            pltpu.VMEM((tokens, tokens), F32),
            pltpu.VMEM((tokens, tokens), F32),
            pltpu.VMEM((tokens, width), F32),
            pltpu.VMEM((tokens, width), F32),
            pltpu.VMEM((2, 2, n, hw), F32),
            pltpu.VMEM((2, n, hw), F32),
            pltpu.VMEM((n, hw), F32),
            pltpu.VMEM((2, n, hw), F32),
            pltpu.VMEM((chips - 1, n, hw), F32),
            pltpu.VMEM((2, 2, n, hw), F32),
            pltpu.VMEM((2, 2, tokens, cols), F32),
            pltpu.VMEM((2, tokens, cols), F32),
            dma((2,)),
            dma((2,)),
            dma((peers - 1,)),
            dma((peers - 1,)),
            dma((2,)),
            dma((2,)),
            dma((chips - 1,)),
            dma((chips - 1,)),
            dma,
            dma,
            dma,
            dma,
        ],
        compiler_params=pltpu.CompilerParams(
            collective_id=0, has_side_effects=True, vmem_limit_bytes=48 << 20
        ),
    )(inputs, log_decay, in_b, in_c, seg_ids.reshape(1, tokens), skip_gain, grad_out)


def solution(mesh):
    return jax.shard_map(
        functools.partial(per_device, mesh.shape["ctx"]),
        mesh=mesh,
        in_specs=(
            P("ctx", "head"),
            P("head", "ctx"),
            P("ctx", "head"),
            P("ctx", "head"),
            P("ctx"),
            P("head"),
            P("ctx", "head"),
        ),
        out_specs=(P("ctx", "head"), P("ctx", "head"), P("ctx", "head"), P("ctx", "head")),
        check_vma=False,
    )
```

```python
import functools

import jax
import jax.numpy as jnp
from jax import lax
from jax.experimental import pallas as pl
from jax.experimental.pallas import tpu as pltpu
from jax.sharding import PartitionSpec as P

MESH = pl.DeviceIdType.MESH
BF = jnp.bfloat16
F32 = jnp.float32
PARTS = 4
VMEM2 = 16 << 20
NT = (((1,), (1,)), ((), ()))
NN = (((1,), (0,)), ((), ()))
TN = (((0,), (0,)), ((), ()))


def mm(a, b, dims=NN):
    return lax.dot_general(a, b, dims, preferred_element_type=F32)


def split(v):
    hi = v.astype(BF)
    return hi, (v - hi.astype(F32)).astype(BF)


def kernel(
    peers, x_hbm, ld_hbm, b_hbm, c_hbm, seg_hbm, skip_hbm, d_hbm,
    ssd_ref, gx_ref, gb_ref, gc_ref,
    x_ref, ld_ref, seg_ref, skip_ref, d_ref, in_sem, bc, info, acum_s, acx, we_s, ws_s, wxh, wxl, wdh, wdl, bias, score_s, dsc,
    ssd_acc, gx_acc, fg, full, half, tbuf, slots, st, gacc, grecv,
    bc_send, bc_recv, i_send, i_recv, d_send, d_recv, t_send, t_recv, s_send, s_recv, g_send, g_recv,
):
    tokens, width = x_hbm.shape
    heads = ld_hbm.shape[0]
    head = width // heads
    hw = width // 2
    pairs = width // 128
    chips = peers // 2
    me = lax.axis_index("ctx")
    hd = lax.axis_index("head")
    side = hd % 2
    mate = hd + 1 - 2 * side
    core = me % 2
    chip = me // 2
    sib = me + 1 - 2 * core

    inputs = [
        pltpu.make_async_copy(src, dst, in_sem.at[k])
        for k, (src, dst) in enumerate((
            (ld_hbm, ld_ref), (seg_hbm, seg_ref), (x_hbm, x_ref), (d_hbm, d_ref), (skip_hbm, skip_ref),
            (b_hbm, bc.at[0, side]), (c_hbm, bc.at[1, side])))
    ]
    for copy in inputs:
        copy.start()

    barrier = pltpu.get_barrier_semaphore()
    for off in range(1, peers):
        pl.semaphore_signal(barrier, inc=1, device_id={"ctx": (me + off) % peers}, device_id_type=MESH)
    pl.semaphore_signal(barrier, inc=1, device_id={"head": mate}, device_id_type=MESH)

    low = lax.broadcasted_iota(jnp.int32, (1, 128), 1) < head
    rows = lax.broadcasted_iota(jnp.int32, (tokens, tokens), 0)
    cols = lax.broadcasted_iota(jnp.int32, (tokens, tokens), 1)
    ones = jnp.where(rows <= cols, 1.0, 0.0).astype(BF)
    inputs[0].wait()
    ld = ld_ref[...]
    l0 = ld.astype(BF)
    r1 = ld - l0.astype(F32)
    l1 = r1.astype(BF)
    l2 = (r1 - l1.astype(F32)).astype(BF)
    acum = mm(l0, ones) + mm(l1, ones) + mm(l2, ones)
    acum_s[...] = acum
    acum_t = jnp.concatenate([acum, jnp.zeros((128 - heads, tokens), F32)], axis=0).T
    for p in range(pairs):
        acx[:, p * 128 : (p + 1) * 128] = jnp.where(
            low, acum_t[:, 2 * p : 2 * p + 1], acum_t[:, 2 * p + 1 : 2 * p + 2]
        )
    inputs[1].wait()
    seg_row = seg_ref[...].astype(F32)
    seg_col = jnp.broadcast_to(seg_row, (128, tokens)).T
    last = jnp.broadcast_to(seg_row[:, tokens - 1 : tokens], (1, hw))
    info[me, 0:1, :] = acx[tokens - 1 : tokens, 0:hw]
    info[me, 1:2, :] = acx[tokens - 1 : tokens, hw:width]
    info[me, 2:3, :] = last
    info[me, 3:4, :] = last

    inputs[2].wait()
    end_mask = jnp.where(seg_col == last[:, 0:128], 1.0, 0.0)
    for p in range(pairs):
        s = slice(p * 128, (p + 1) * 128)
        a = acx[:, s]
        we = jnp.exp(a[tokens - 1 : tokens, :] - a) * end_mask
        we_s[:, s] = we
        hi, lo = split(x_ref[:, s].astype(F32) * we)
        wxh[:, s] = hi
        wxl[:, s] = lo

    pl.semaphore_wait(barrier, peers)

    bc_copies = []
    for k, ref in enumerate((b_hbm, c_hbm)):
        copy = pltpu.make_async_remote_copy(
            src_ref=ref, dst_ref=bc.at[k, side], send_sem=bc_send.at[k], recv_sem=bc_recv.at[k],
            device_id={"head": mate}, device_id_type=MESH)
        copy.start()
        bc_copies.append(copy)
    i_copies = []
    for off in range(1, peers):
        copy = pltpu.make_async_remote_copy(
            src_ref=info.at[me], dst_ref=info.at[me], send_sem=i_send.at[off - 1], recv_sem=i_recv.at[off - 1],
            device_id={"ctx": (me + off) % peers}, device_id_type=MESH)
        copy.start()
        i_copies.append(copy)

    for off in range(1, peers):
        src = (me + peers - off) % peers
        pltpu.make_async_remote_copy(
            src_ref=info.at[src], dst_ref=info.at[src], send_sem=i_send.at[off - 1], recv_sem=i_recv.at[off - 1],
            device_id={"ctx": (me + off) % peers}, device_id_type=MESH).wait_recv()

    def seg_of(i):
        return info[(i + peers) % peers, 2:3, :]

    def prev_seg(i):
        return jnp.where(i == 0, -1.0, seg_of(i - 1))

    inputs[3].wait()
    start_mask = jnp.where(seg_col == prev_seg(me)[:, 0:128], 1.0, 0.0)
    for p in range(pairs):
        s = slice(p * 128, (p + 1) * 128)
        ws = jnp.exp(acx[:, s]) * start_mask
        ws_s[:, s] = ws
        hi, lo = split(d_ref[:, s].astype(F32) * ws)
        wdh[:, s] = hi
        wdl[:, s] = lo

    for copy in bc_copies:
        copy.wait_recv()
    inputs[5].wait()
    inputs[6].wait()
    b_full = jnp.concatenate([bc[0, 0], bc[0, 1]], axis=1)
    c_full = jnp.concatenate([bc[1, 0], bc[1, 1]], axis=1)
    b_t = b_full.T
    c_t = c_full.T
    def carry(i, k):
        return jnp.exp(info[i, pl.ds(k, 1), :]) * jnp.where(seg_of(i) == prev_seg(i), 1.0, 0.0)

    parts = fg.shape[0]
    cw = fg.shape[4]
    d_copies = []
    for q in range(parts):
        for k in range(2):
            s = slice(k * hw + q * cw, k * hw + (q + 1) * cw)
            fg[q, 0, k] = mm(b_t, wxh[:, s]) + mm(b_t, wxl[:, s])
            fg[q, 1, k] = mm(c_t, wdh[:, s]) + mm(c_t, wdl[:, s])
        half_copy = pltpu.make_async_remote_copy(
            src_ref=fg.at[q, 1 - core, 1 - core], dst_ref=half.at[q],
            send_sem=d_send.at[2 * q], recv_sem=d_recv.at[2 * q],
            device_id={"ctx": sib}, device_id_type=MESH)
        half_copy.start()
        full_copy = pltpu.make_async_remote_copy(
            src_ref=fg.at[q, core], dst_ref=full.at[q],
            send_sem=d_send.at[2 * q + 1], recv_sem=d_recv.at[2 * q + 1],
            device_id={"ctx": sib}, device_id_type=MESH)
        full_copy.start()
        d_copies += [half_copy, full_copy]

    sib_carry = carry(sib, core)
    my_carry = carry(me, core)
    t_copies = []
    for q in range(parts):
        u = slice(q * cw, (q + 1) * cw)
        d_copies[2 * q].wait_recv()
        tbuf[q, core] = half[q] + sib_carry[:, u] * fg[q, core, core]
        d_copies[2 * q + 1].wait_recv()
        tbuf[q, 1 - core] = fg[q, 1 - core, core] + my_carry[:, u] * full[q, core]
        for off in range(1, chips):
            at = q * (chips - 1) + off - 1
            copy = pltpu.make_async_remote_copy(
                src_ref=tbuf.at[q, (chip + off) // chips], dst_ref=slots.at[at],
                send_sem=t_send.at[at], recv_sem=t_recv.at[at],
                device_id={"ctx": ((chip + off) % chips) * 2 + core}, device_id_type=MESH)
            copy.start()
            t_copies.append(copy)

    bias[...] = jnp.where(
        (rows >= cols) & (jnp.concatenate([seg_col] * (tokens // 128), axis=1) == seg_row), 0.0, -1e30
    )
    inputs[4].wait()
    score_s[...] = mm(c_full, b_full, NT)
    dsc[...] = jnp.zeros_like(dsc)

    def pair_step(p, carried):
        s = pl.ds(pl.multiple_of(p * 128, 128), 128)
        x = x_ref[:, s]
        d = d_ref[:, s]
        gain = jnp.where(low, skip_ref[2 * p], skip_ref[2 * p + 1])
        out = gain * x.astype(F32)
        gx = gain * d.astype(F32)
        zero = jnp.zeros_like(x)
        total = dsc[...]
        for k in range(2):
            mine = low if k == 0 else jnp.logical_not(low)
            xm = jnp.where(mine, x, zero)
            dm = jnp.where(mine, d, zero)
            a_col = acx[:, s][:, k * head : k * head + 1]
            a_row = acum_s[pl.ds(2 * p + k, 1), :]
            table = jnp.exp((a_col - a_row) + bias[...])
            mixed = (table * score_s[...]).astype(BF)
            out = out + mm(mixed, xm)
            gx = gx + mm(mixed, dm, TN)
            total = total + mm(dm, x, NT) * table
        dsc[...] = total
        ssd_acc[:, s] = out
        gx_acc[:, s] = gx
        return carried

    lax.fori_loop(0, pairs, pair_step, 0)

    ds_hi, ds_lo = split(dsc[...])
    gb = mm(ds_hi, c_full, TN) + mm(ds_lo, c_full, TN)
    gc = mm(ds_hi, b_full) + mm(ds_lo, b_full)

    weights = []
    for off in range(1, chips):
        src = (chip + chips - off) % chips
        first = jnp.minimum(src, chip)
        final = jnp.maximum(src, chip)
        total = jnp.zeros((1, hw), F32)
        for i in range(peers):
            within = (i >= 2 * first + 2) & (i < 2 * final)
            total = total + jnp.where(within, info[i, pl.ds(core, 1), :], 0.0)
        weights.append(jnp.exp(total) * jnp.where(seg_of(2 * first + 1) == seg_of(2 * final - 1), 1.0, 0.0))
    sib_both = [carry(sib, k) for k in range(2)]

    def gather(q):
        u = slice(q * cw, (q + 1) * cw)
        st[q, core, 0] = jnp.zeros(st.shape[3:], F32)
        st[q, core, 1] = jnp.zeros(st.shape[3:], F32)
        for off in range(1, chips):
            later = 1 - (chip + chips - off) // chips
            at = q * (chips - 1) + off - 1
            t_copies[at].wait_recv()
            st[q, core, later] = st[q, core, later] + weights[off - 1][:, u] * slots[at]
        copy = pltpu.make_async_remote_copy(
            src_ref=st.at[q, core], dst_ref=st.at[q, core], send_sem=s_send.at[q], recv_sem=s_recv.at[q],
            device_id={"ctx": sib}, device_id_type=MESH)
        copy.start()
        return copy

    def absorb(q, copy, gb, gc):
        u = slice(q * cw, (q + 1) * cw)
        copy.wait_send()
        pltpu.make_async_remote_copy(
            src_ref=st.at[q, 1 - core], dst_ref=st.at[q, 1 - core], send_sem=s_send.at[q], recv_sem=s_recv.at[q],
            device_id={"ctx": sib}, device_id_type=MESH).wait_recv()
        for k in range(2):
            s = slice(k * hw + q * cw, k * hw + (q + 1) * cw)
            st[q, k, 1 - core] = sib_both[k][:, u] * st[q, k, 1 - core] + full[q, k]
            s_hi, s_lo = split(st[q, k, 0])
            a_hi, a_lo = split(st[q, k, 1])
            gb = gb + mm(wxh[:, s], a_hi, NT) + mm(wxl[:, s], a_hi, NT) + mm(wxh[:, s], a_lo, NT)
            gc = gc + mm(wdh[:, s], s_hi, NT) + mm(wdl[:, s], s_hi, NT) + mm(wdh[:, s], s_lo, NT)
        return gb, gc

    def outputs(q):
        for k in range(2):
            s = slice(k * hw + q * cw, k * hw + (q + 1) * cw)
            s_hi, s_lo = split(st[q, k, 0])
            a_hi, a_lo = split(st[q, k, 1])
            ssd_ref[:, s] = (ssd_acc[:, s] + ws_s[:, s] * (mm(c_full, s_hi) + mm(c_full, s_lo))).astype(BF)
            gx_ref[:, s] = (gx_acc[:, s] + we_s[:, s] * (mm(b_full, a_hi) + mm(b_full, a_lo))).astype(BF)

    s_copy = gather(0)
    for q in range(parts):
        here = s_copy
        if q + 1 < parts:
            gb, gc = absorb(q, here, gb, gc)
            outputs(q)
            s_copy = gather(q + 1)
        else:
            gb, gc = absorb(q, here, gb, gc)
    n = gb.shape[1] // 2
    for k in range(2):
        gacc[k, 0] = gb[:, k * n : (k + 1) * n]
        gacc[k, 1] = gc[:, k * n : (k + 1) * n]
    g_copy = pltpu.make_async_remote_copy(
        src_ref=gacc.at[1 - side], dst_ref=grecv, send_sem=g_send, recv_sem=g_recv,
        device_id={"head": mate}, device_id_type=MESH)
    g_copy.start()

    outputs(parts - 1)

    g_copy.wait_recv()
    gb_ref[...] = (gacc[side, 0] + grecv[0]).astype(BF)
    gc_ref[...] = (gacc[side, 1] + grecv[1]).astype(BF)

    for copy in bc_copies + i_copies + d_copies + t_copies + [g_copy]:
        copy.wait_send()


def per_device(peers, inputs, log_decay, in_b, in_c, seg_ids, skip_gain, grad_out):
    tokens, width = inputs.shape
    heads = log_decay.shape[0]
    cols = in_b.shape[1]
    n = 2 * cols
    hw = width // 2
    chips = peers // 2
    cw = hw // PARTS
    vm = pl.BlockSpec(memory_space=pltpu.VMEM)
    dma = pltpu.SemaphoreType.DMA
    results = pl.pallas_call(
        functools.partial(kernel, peers),
        out_shape=(
            jax.ShapeDtypeStruct((tokens, width), BF),
            jax.ShapeDtypeStruct((tokens, width), BF),
            jax.ShapeDtypeStruct((tokens, cols), BF),
            jax.ShapeDtypeStruct((tokens, cols), BF),
        ),
        in_specs=[pl.BlockSpec(memory_space=pltpu.HBM)] * 7,
        out_specs=(vm, vm, vm, vm),
        scratch_shapes=[
            pltpu.VMEM((tokens, width), BF),
            pltpu.VMEM((heads, tokens), F32),
            pltpu.VMEM((1, tokens), jnp.int32),
            pltpu.SMEM((heads,), F32),
            pltpu.VMEM((tokens, width), BF),
            dma((7,)),
            pltpu.VMEM((2, 2, tokens, cols), BF),
            pltpu.VMEM((peers, 4, hw), F32),
            pltpu.VMEM((heads, tokens), F32),
            pltpu.VMEM((tokens, width), F32),
            pltpu.VMEM((tokens, width), F32),
            pltpu.VMEM((tokens, width), F32),
            pltpu.VMEM((tokens, width), BF),
            pltpu.VMEM((tokens, width), BF),
            pltpu.VMEM((tokens, width), BF),
            pltpu.VMEM((tokens, width), BF),
            pltpu.VMEM((tokens, tokens), F32),
            pltpu.VMEM((tokens, tokens), F32),
            pltpu.VMEM((tokens, tokens), F32),
            pltpu.VMEM((tokens, width), F32),
            pltpu.VMEM((tokens, width), F32),
            pltpu.VMEM((PARTS, 2, 2, n, cw), F32),
            pltpu.VMEM((PARTS, 2, n, cw), F32),
            pltpu.VMEM((PARTS, n, cw), F32),
            pltpu.VMEM((PARTS, 2, n, cw), F32),
            pltpu.VMEM((PARTS * (chips - 1), n, cw), F32),
            pltpu.VMEM((PARTS, 2, 2, n, cw), F32),
            pltpu.VMEM((2, 2, tokens, cols), F32),
            pltpu.VMEM((2, tokens, cols), F32),
            dma((2,)),
            dma((2,)),
            dma((peers - 1,)),
            dma((peers - 1,)),
            dma((2 * PARTS,)),
            dma((2 * PARTS,)),
            dma((PARTS * (chips - 1),)),
            dma((PARTS * (chips - 1),)),
            dma((PARTS,)),
            dma((PARTS,)),
            dma,
            dma,
        ],
        compiler_params=pltpu.CompilerParams(
            collective_id=0, has_side_effects=True, vmem_limit_bytes=48 << 20
        ),
    )(*[pltpu.with_memory_space_constraint(a, pltpu.HBM) for a in (inputs, log_decay, in_b, in_c, seg_ids.reshape(1, tokens), skip_gain, grad_out)])
    hbm = pl.BlockSpec(memory_space=pltpu.HBM)
    return pl.pallas_call(
        hand_over,
        out_shape=tuple(jax.ShapeDtypeStruct(r.shape, r.dtype) for r in results),
        in_specs=[hbm] * 4,
        out_specs=(hbm,) * 4,
        scratch_shapes=[dma((4,))],
        compiler_params=pltpu.CompilerParams(vmem_limit_bytes=VMEM2),
    )(*results)


def hand_over(a, b, c, d, out_a, out_b, out_c, out_d, sem):
    copies = [
        pltpu.make_async_copy(src, dst, sem.at[k])
        for k, (src, dst) in enumerate(((a, out_a), (b, out_b), (c, out_c), (d, out_d)))
    ]
    for copy in copies:
        copy.start()
    for copy in copies:
        copy.wait()


def solution(mesh):
    return jax.shard_map(
        functools.partial(per_device, mesh.shape["ctx"]),
        mesh=mesh,
        in_specs=(
            P("ctx", "head"),
            P("head", "ctx"),
            P("ctx", "head"),
            P("ctx", "head"),
            P("ctx"),
            P("head"),
            P("ctx", "head"),
        ),
        out_specs=(P("ctx", "head"), P("ctx", "head"), P("ctx", "head"), P("ctx", "head")),
        check_vma=False,
    )
```

```python
import functools

import jax
import jax.numpy as jnp
from jax import lax
from jax.experimental import pallas as pl
from jax.experimental.pallas import tpu as pltpu
from jax.sharding import PartitionSpec as P

MESH = pl.DeviceIdType.MESH
BF = jnp.bfloat16
F32 = jnp.float32
PARTS = 4
VMEM2 = 16 << 20
NT = (((1,), (1,)), ((), ()))
NN = (((1,), (0,)), ((), ()))
TN = (((0,), (0,)), ((), ()))


def mm(a, b, dims=NN):
    return lax.dot_general(a, b, dims, preferred_element_type=F32)


def split(v):
    hi = v.astype(BF)
    return hi, (v - hi.astype(F32)).astype(BF)


def kernel(
    peers, x_hbm, ld_hbm, b_hbm, c_hbm, seg_hbm, skip_hbm, d_hbm,
    ssd_ref, gx_ref, gb_ref, gc_ref,
    x_ref, ld_ref, seg_ref, skip_ref, d_ref, in_sem, bc, info, acum_s, acx, we_s, ws_s, wxh, wxl, wdh, wdl, bias, score_s, dsc,
    ssd_acc, gx_acc, fg, full, half, tbuf, slots, st, gacc, grecv,
    bc_send, bc_recv, i_send, i_recv, d_send, d_recv, t_send, t_recv, s_send, s_recv, g_send, g_recv,
):
    tokens, width = x_hbm.shape
    heads = ld_hbm.shape[0]
    head = width // heads
    hw = width // 2
    pairs = width // 128
    chips = peers // 2
    me = lax.axis_index("ctx")
    hd = lax.axis_index("head")
    side = hd % 2
    mate = hd + 1 - 2 * side
    core = me % 2
    chip = me // 2
    sib = me + 1 - 2 * core

    inputs = [
        pltpu.make_async_copy(src, dst, in_sem.at[k])
        for k, (src, dst) in enumerate((
            (ld_hbm, ld_ref), (seg_hbm, seg_ref), (x_hbm, x_ref), (d_hbm, d_ref), (skip_hbm, skip_ref),
            (b_hbm, bc.at[0, side]), (c_hbm, bc.at[1, side])))
    ]
    for copy in inputs:
        copy.start()

    barrier = pltpu.get_barrier_semaphore()
    for off in range(1, peers):
        pl.semaphore_signal(barrier, inc=1, device_id={"ctx": (me + off) % peers}, device_id_type=MESH)
    pl.semaphore_signal(barrier, inc=1, device_id={"head": mate}, device_id_type=MESH)

    low = lax.broadcasted_iota(jnp.int32, (1, 128), 1) < head
    rows = lax.broadcasted_iota(jnp.int32, (tokens, tokens), 0)
    cols = lax.broadcasted_iota(jnp.int32, (tokens, tokens), 1)
    ones = jnp.where(rows <= cols, 1.0, 0.0).astype(BF)
    inputs[0].wait()
    ld = ld_ref[...]
    l0 = ld.astype(BF)
    r1 = ld - l0.astype(F32)
    l1 = r1.astype(BF)
    l2 = (r1 - l1.astype(F32)).astype(BF)
    acum = mm(l0, ones) + mm(l1, ones) + mm(l2, ones)
    acum_s[...] = acum
    acum_t = jnp.concatenate([acum, jnp.zeros((128 - heads, tokens), F32)], axis=0).T
    for p in range(pairs):
        acx[:, p * 128 : (p + 1) * 128] = jnp.where(
            low, acum_t[:, 2 * p : 2 * p + 1], acum_t[:, 2 * p + 1 : 2 * p + 2]
        )
    inputs[1].wait()
    seg_row = seg_ref[...].astype(F32)
    seg_col = jnp.broadcast_to(seg_row, (128, tokens)).T
    last = jnp.broadcast_to(seg_row[:, tokens - 1 : tokens], (1, hw))
    info[me, 0:1, :] = acx[tokens - 1 : tokens, 0:hw]
    info[me, 1:2, :] = acx[tokens - 1 : tokens, hw:width]
    info[me, 2:3, :] = last
    info[me, 3:4, :] = last

    inputs[2].wait()
    end_mask = jnp.where(seg_col == last[:, 0:128], 1.0, 0.0)
    for p in range(pairs):
        s = slice(p * 128, (p + 1) * 128)
        a = acx[:, s]
        we = jnp.exp(a[tokens - 1 : tokens, :] - a) * end_mask
        we_s[:, s] = we
        hi, lo = split(x_ref[:, s].astype(F32) * we)
        wxh[:, s] = hi
        wxl[:, s] = lo

    pl.semaphore_wait(barrier, peers)

    bc_copies = []
    for k, ref in enumerate((b_hbm, c_hbm)):
        copy = pltpu.make_async_remote_copy(
            src_ref=ref, dst_ref=bc.at[k, side], send_sem=bc_send.at[k], recv_sem=bc_recv.at[k],
            device_id={"head": mate}, device_id_type=MESH)
        copy.start()
        bc_copies.append(copy)
    i_copies = []
    for off in range(1, peers):
        copy = pltpu.make_async_remote_copy(
            src_ref=info.at[me], dst_ref=info.at[me], send_sem=i_send.at[off - 1], recv_sem=i_recv.at[off - 1],
            device_id={"ctx": (me + off) % peers}, device_id_type=MESH)
        copy.start()
        i_copies.append(copy)

    for off in range(1, peers):
        src = (me + peers - off) % peers
        pltpu.make_async_remote_copy(
            src_ref=info.at[src], dst_ref=info.at[src], send_sem=i_send.at[off - 1], recv_sem=i_recv.at[off - 1],
            device_id={"ctx": (me + off) % peers}, device_id_type=MESH).wait_recv()

    def seg_of(i):
        return info[(i + peers) % peers, 2:3, :]

    def prev_seg(i):
        return jnp.where(i == 0, -1.0, seg_of(i - 1))

    inputs[3].wait()
    start_mask = jnp.where(seg_col == prev_seg(me)[:, 0:128], 1.0, 0.0)
    for p in range(pairs):
        s = slice(p * 128, (p + 1) * 128)
        ws = jnp.exp(acx[:, s]) * start_mask
        ws_s[:, s] = ws
        hi, lo = split(d_ref[:, s].astype(F32) * ws)
        wdh[:, s] = hi
        wdl[:, s] = lo

    for copy in bc_copies:
        copy.wait_recv()
    inputs[5].wait()
    inputs[6].wait()
    b_full = jnp.concatenate([bc[0, 0], bc[0, 1]], axis=1)
    c_full = jnp.concatenate([bc[1, 0], bc[1, 1]], axis=1)
    b_t = b_full.T
    c_t = c_full.T
    def carry(i, k):
        return jnp.exp(info[i, pl.ds(k, 1), :]) * jnp.where(seg_of(i) == prev_seg(i), 1.0, 0.0)

    parts = fg.shape[0]
    cw = fg.shape[4]
    sib_carry = carry(sib, core)
    my_carry = carry(me, core)
    d_copies = []
    t_copies = []

    def forward(q):
        u = slice(q * cw, (q + 1) * cw)
        d_copies[2 * q].wait_recv()
        tbuf[q, core] = half[q] + sib_carry[:, u] * fg[q, core, core]
        d_copies[2 * q + 1].wait_recv()
        tbuf[q, 1 - core] = fg[q, 1 - core, core] + my_carry[:, u] * full[q, core]
        for off in range(1, chips):
            at = q * (chips - 1) + off - 1
            copy = pltpu.make_async_remote_copy(
                src_ref=tbuf.at[q, (chip + off) // chips], dst_ref=slots.at[at],
                send_sem=t_send.at[at], recv_sem=t_recv.at[at],
                device_id={"ctx": ((chip + off) % chips) * 2 + core}, device_id_type=MESH)
            copy.start()
            t_copies.append(copy)

    for q in range(parts):
        for k in range(2):
            s = slice(k * hw + q * cw, k * hw + (q + 1) * cw)
            fg[q, 0, k] = mm(b_t, wxh[:, s]) + mm(b_t, wxl[:, s])
            fg[q, 1, k] = mm(c_t, wdh[:, s]) + mm(c_t, wdl[:, s])
        half_copy = pltpu.make_async_remote_copy(
            src_ref=fg.at[q, 1 - core, 1 - core], dst_ref=half.at[q],
            send_sem=d_send.at[2 * q], recv_sem=d_recv.at[2 * q],
            device_id={"ctx": sib}, device_id_type=MESH)
        half_copy.start()
        full_copy = pltpu.make_async_remote_copy(
            src_ref=fg.at[q, core], dst_ref=full.at[q],
            send_sem=d_send.at[2 * q + 1], recv_sem=d_recv.at[2 * q + 1],
            device_id={"ctx": sib}, device_id_type=MESH)
        full_copy.start()
        d_copies += [half_copy, full_copy]
        if q:
            forward(q - 1)
    forward(parts - 1)


    bias[...] = jnp.where(
        (rows >= cols) & (jnp.concatenate([seg_col] * (tokens // 128), axis=1) == seg_row), 0.0, -1e30
    )
    inputs[4].wait()
    score_s[...] = mm(c_full, b_full, NT)
    dsc[...] = jnp.zeros_like(dsc)

    def pair_step(p, carried):
        s = pl.ds(pl.multiple_of(p * 128, 128), 128)
        x = x_ref[:, s]
        d = d_ref[:, s]
        gain = jnp.where(low, skip_ref[2 * p], skip_ref[2 * p + 1])
        out = gain * x.astype(F32)
        gx = gain * d.astype(F32)
        zero = jnp.zeros_like(x)
        total = dsc[...]
        for k in range(2):
            mine = low if k == 0 else jnp.logical_not(low)
            xm = jnp.where(mine, x, zero)
            dm = jnp.where(mine, d, zero)
            a_col = acx[:, s][:, k * head : k * head + 1]
            a_row = acum_s[pl.ds(2 * p + k, 1), :]
            table = jnp.exp((a_col - a_row) + bias[...])
            mixed = (table * score_s[...]).astype(BF)
            out = out + mm(mixed, xm)
            gx = gx + mm(mixed, dm, TN)
            total = total + mm(dm, x, NT) * table
        dsc[...] = total
        ssd_acc[:, s] = out
        gx_acc[:, s] = gx
        return carried

    lax.fori_loop(0, pairs, pair_step, 0)

    ds_hi, ds_lo = split(dsc[...])
    gb = mm(ds_hi, c_full, TN) + mm(ds_lo, c_full, TN)
    gc = mm(ds_hi, b_full) + mm(ds_lo, b_full)

    weights = []
    for off in range(1, chips):
        src = (chip + chips - off) % chips
        first = jnp.minimum(src, chip)
        final = jnp.maximum(src, chip)
        total = jnp.zeros((1, hw), F32)
        for i in range(peers):
            within = (i >= 2 * first + 2) & (i < 2 * final)
            total = total + jnp.where(within, info[i, pl.ds(core, 1), :], 0.0)
        weights.append(jnp.exp(total) * jnp.where(seg_of(2 * first + 1) == seg_of(2 * final - 1), 1.0, 0.0))
    sib_both = [carry(sib, k) for k in range(2)]

    def gather(q):
        u = slice(q * cw, (q + 1) * cw)
        st[q, core, 0] = jnp.zeros(st.shape[3:], F32)
        st[q, core, 1] = jnp.zeros(st.shape[3:], F32)
        for off in range(1, chips):
            later = 1 - (chip + chips - off) // chips
            at = q * (chips - 1) + off - 1
            t_copies[at].wait_recv()
            st[q, core, later] = st[q, core, later] + weights[off - 1][:, u] * slots[at]
        copy = pltpu.make_async_remote_copy(
            src_ref=st.at[q, core], dst_ref=st.at[q, core], send_sem=s_send.at[q], recv_sem=s_recv.at[q],
            device_id={"ctx": sib}, device_id_type=MESH)
        copy.start()
        return copy

    n = b_full.shape[1] // 2
    g_copies = []

    def send_off(which, grad):
        for k in range(2):
            gacc[k, which] = grad[:, k * n : (k + 1) * n]
        g_copy = pltpu.make_async_remote_copy(
            src_ref=gacc.at[1 - side, which], dst_ref=grecv.at[which],
            send_sem=g_send.at[which], recv_sem=g_recv.at[which],
            device_id={"head": mate}, device_id_type=MESH)
        g_copy.start()
        g_copies.append(g_copy)

    def absorb(q, copy, gb, gc):
        u = slice(q * cw, (q + 1) * cw)
        copy.wait_send()
        pltpu.make_async_remote_copy(
            src_ref=st.at[q, 1 - core], dst_ref=st.at[q, 1 - core], send_sem=s_send.at[q], recv_sem=s_recv.at[q],
            device_id={"ctx": sib}, device_id_type=MESH).wait_recv()
        for k in range(2):
            s = slice(k * hw + q * cw, k * hw + (q + 1) * cw)
            st[q, k, 1 - core] = sib_both[k][:, u] * st[q, k, 1 - core] + full[q, k]
            a_hi, a_lo = split(st[q, k, 1])
            gb = gb + mm(wxh[:, s], a_hi, NT) + mm(wxl[:, s], a_hi, NT) + mm(wxh[:, s], a_lo, NT)
        if q == parts - 1:
            send_off(0, gb)
        for k in range(2):
            s = slice(k * hw + q * cw, k * hw + (q + 1) * cw)
            s_hi, s_lo = split(st[q, k, 0])
            gc = gc + mm(wdh[:, s], s_hi, NT) + mm(wdl[:, s], s_hi, NT) + mm(wdh[:, s], s_lo, NT)
        if q == parts - 1:
            send_off(1, gc)
        return gb, gc

    def outputs(q):
        for k in range(2):
            s = slice(k * hw + q * cw, k * hw + (q + 1) * cw)
            s_hi, s_lo = split(st[q, k, 0])
            a_hi, a_lo = split(st[q, k, 1])
            ssd_ref[:, s] = (ssd_acc[:, s] + ws_s[:, s] * (mm(c_full, s_hi) + mm(c_full, s_lo))).astype(BF)
            gx_ref[:, s] = (gx_acc[:, s] + we_s[:, s] * (mm(b_full, a_hi) + mm(b_full, a_lo))).astype(BF)

    s_copy = gather(0)
    for q in range(parts):
        here = s_copy
        if q + 1 < parts:
            gb, gc = absorb(q, here, gb, gc)
            outputs(q)
            s_copy = gather(q + 1)
        else:
            gb, gc = absorb(q, here, gb, gc)
    outputs(parts - 1)

    g_copies[0].wait_recv()
    gb_ref[...] = (gacc[side, 0] + grecv[0]).astype(BF)
    g_copies[1].wait_recv()
    gc_ref[...] = (gacc[side, 1] + grecv[1]).astype(BF)

    for copy in bc_copies + i_copies + d_copies + t_copies + g_copies:
        copy.wait_send()


def per_device(peers, inputs, log_decay, in_b, in_c, seg_ids, skip_gain, grad_out):
    tokens, width = inputs.shape
    heads = log_decay.shape[0]
    cols = in_b.shape[1]
    n = 2 * cols
    hw = width // 2
    chips = peers // 2
    cw = hw // PARTS
    vm = pl.BlockSpec(memory_space=pltpu.VMEM)
    dma = pltpu.SemaphoreType.DMA
    results = pl.pallas_call(
        functools.partial(kernel, peers),
        out_shape=(
            jax.ShapeDtypeStruct((tokens, width), BF),
            jax.ShapeDtypeStruct((tokens, width), BF),
            jax.ShapeDtypeStruct((tokens, cols), BF),
            jax.ShapeDtypeStruct((tokens, cols), BF),
        ),
        in_specs=[pl.BlockSpec(memory_space=pltpu.HBM)] * 7,
        out_specs=(vm, vm, vm, vm),
        scratch_shapes=[
            pltpu.VMEM((tokens, width), BF),
            pltpu.VMEM((heads, tokens), F32),
            pltpu.VMEM((1, tokens), jnp.int32),
            pltpu.SMEM((heads,), F32),
            pltpu.VMEM((tokens, width), BF),
            dma((7,)),
            pltpu.VMEM((2, 2, tokens, cols), BF),
            pltpu.VMEM((peers, 4, hw), F32),
            pltpu.VMEM((heads, tokens), F32),
            pltpu.VMEM((tokens, width), F32),
            pltpu.VMEM((tokens, width), F32),
            pltpu.VMEM((tokens, width), F32),
            pltpu.VMEM((tokens, width), BF),
            pltpu.VMEM((tokens, width), BF),
            pltpu.VMEM((tokens, width), BF),
            pltpu.VMEM((tokens, width), BF),
            pltpu.VMEM((tokens, tokens), F32),
            pltpu.VMEM((tokens, tokens), F32),
            pltpu.VMEM((tokens, tokens), F32),
            pltpu.VMEM((tokens, width), F32),
            pltpu.VMEM((tokens, width), F32),
            pltpu.VMEM((PARTS, 2, 2, n, cw), F32),
            pltpu.VMEM((PARTS, 2, n, cw), F32),
            pltpu.VMEM((PARTS, n, cw), F32),
            pltpu.VMEM((PARTS, 2, n, cw), F32),
            pltpu.VMEM((PARTS * (chips - 1), n, cw), F32),
            pltpu.VMEM((PARTS, 2, 2, n, cw), F32),
            pltpu.VMEM((2, 2, tokens, cols), F32),
            pltpu.VMEM((2, tokens, cols), F32),
            dma((2,)),
            dma((2,)),
            dma((peers - 1,)),
            dma((peers - 1,)),
            dma((2 * PARTS,)),
            dma((2 * PARTS,)),
            dma((PARTS * (chips - 1),)),
            dma((PARTS * (chips - 1),)),
            dma((PARTS,)),
            dma((PARTS,)),
            dma((2,)),
            dma((2,)),
        ],
        compiler_params=pltpu.CompilerParams(
            collective_id=0, has_side_effects=True, vmem_limit_bytes=48 << 20
        ),
    )(*[pltpu.with_memory_space_constraint(a, pltpu.HBM) for a in (inputs, log_decay, in_b, in_c, seg_ids.reshape(1, tokens), skip_gain, grad_out)])
    hbm = pl.BlockSpec(memory_space=pltpu.HBM)
    return pl.pallas_call(
        hand_over,
        out_shape=tuple(jax.ShapeDtypeStruct(r.shape, r.dtype) for r in results),
        in_specs=[hbm] * 4,
        out_specs=(hbm,) * 4,
        scratch_shapes=[dma((4,))],
        compiler_params=pltpu.CompilerParams(vmem_limit_bytes=VMEM2),
    )(*results)


def hand_over(a, b, c, d, out_a, out_b, out_c, out_d, sem):
    copies = [
        pltpu.make_async_copy(src, dst, sem.at[k])
        for k, (src, dst) in enumerate(((a, out_a), (b, out_b), (c, out_c), (d, out_d)))
    ]
    for copy in copies:
        copy.start()
    for copy in copies:
        copy.wait()


def solution(mesh):
    return jax.shard_map(
        functools.partial(per_device, mesh.shape["ctx"]),
        mesh=mesh,
        in_specs=(
            P("ctx", "head"),
            P("head", "ctx"),
            P("ctx", "head"),
            P("ctx", "head"),
            P("ctx"),
            P("head"),
            P("ctx", "head"),
        ),
        out_specs=(P("ctx", "head"), P("ctx", "head"), P("ctx", "head"), P("ctx", "head")),
        check_vma=False,
    )
```

```python
import functools

import jax
import jax.numpy as jnp
from jax import lax
from jax.experimental import pallas as pl
from jax.experimental.pallas import tpu as pltpu
from jax.sharding import PartitionSpec as P

MESH = pl.DeviceIdType.MESH
BF = jnp.bfloat16
F32 = jnp.float32
PARTS = 4
VMEM2 = 16 << 20
NT = (((1,), (1,)), ((), ()))
NN = (((1,), (0,)), ((), ()))
TN = (((0,), (0,)), ((), ()))


def mm(a, b, dims=NN):
    return lax.dot_general(a, b, dims, preferred_element_type=F32)


def split(v):
    hi = v.astype(BF)
    return hi, (v - hi.astype(F32)).astype(BF)


def kernel(
    peers, x_hbm, ld_hbm, b_hbm, c_hbm, seg_hbm, skip_hbm, d_hbm,
    ssd_ref, gx_ref, gb_ref, gc_ref,
    x_ref, ld_ref, seg_ref, skip_ref, d_ref, in_sem, bc, info, acum_s, acx, we_s, ws_s, wxh, wxl, wdh, wdl, bias, score_s, dsc,
    ssd_acc, gx_acc, fg, full, half, tbuf, slots, st, gacc, grecv,
    bc_send, bc_recv, i_send, i_recv, d_send, d_recv, t_send, t_recv, s_send, s_recv, g_send, g_recv,
):
    tokens, width = x_hbm.shape
    heads = ld_hbm.shape[0]
    head = width // heads
    hw = width // 2
    pairs = width // 128
    chips = peers // 2
    me = lax.axis_index("ctx")
    hd = lax.axis_index("head")
    side = hd % 2
    mate = hd + 1 - 2 * side
    core = me % 2
    chip = me // 2
    sib = me + 1 - 2 * core

    inputs = [
        pltpu.make_async_copy(src, dst, in_sem.at[k])
        for k, (src, dst) in enumerate((
            (ld_hbm, ld_ref), (seg_hbm, seg_ref), (x_hbm, x_ref), (d_hbm, d_ref), (skip_hbm, skip_ref),
            (b_hbm, bc.at[0, side]), (c_hbm, bc.at[1, side])))
    ]
    for copy in inputs:
        copy.start()

    barrier = pltpu.get_barrier_semaphore()
    for off in range(1, peers):
        pl.semaphore_signal(barrier, inc=1, device_id={"ctx": (me + off) % peers}, device_id_type=MESH)
    pl.semaphore_signal(barrier, inc=1, device_id={"head": mate}, device_id_type=MESH)

    low = lax.broadcasted_iota(jnp.int32, (1, 128), 1) < head
    rows = lax.broadcasted_iota(jnp.int32, (tokens, tokens), 0)
    cols = lax.broadcasted_iota(jnp.int32, (tokens, tokens), 1)
    ones = jnp.where(rows <= cols, 1.0, 0.0).astype(BF)
    inputs[0].wait()
    ld = ld_ref[...]
    l0 = ld.astype(BF)
    r1 = ld - l0.astype(F32)
    l1 = r1.astype(BF)
    l2 = (r1 - l1.astype(F32)).astype(BF)
    acum = mm(l0, ones) + mm(l1, ones) + mm(l2, ones)
    acum_s[...] = acum
    acum_t = jnp.concatenate([acum, jnp.zeros((128 - heads, tokens), F32)], axis=0).T
    for p in range(pairs):
        acx[:, p * 128 : (p + 1) * 128] = jnp.where(
            low, acum_t[:, 2 * p : 2 * p + 1], acum_t[:, 2 * p + 1 : 2 * p + 2]
        )
    inputs[1].wait()
    seg_row = seg_ref[...].astype(F32)
    seg_col = jnp.broadcast_to(seg_row, (128, tokens)).T
    last = jnp.broadcast_to(seg_row[:, tokens - 1 : tokens], (1, hw))
    info[me, 0:1, :] = acx[tokens - 1 : tokens, 0:hw]
    info[me, 1:2, :] = acx[tokens - 1 : tokens, hw:width]
    info[me, 2:3, :] = last
    info[me, 3:4, :] = last

    inputs[2].wait()
    end_mask = jnp.where(seg_col == last[:, 0:128], 1.0, 0.0)
    for p in range(pairs):
        s = slice(p * 128, (p + 1) * 128)
        a = acx[:, s]
        we = jnp.exp(a[tokens - 1 : tokens, :] - a) * end_mask
        we_s[:, s] = we
        hi, lo = split(x_ref[:, s].astype(F32) * we)
        wxh[:, s] = hi
        wxl[:, s] = lo

    pl.semaphore_wait(barrier, peers)

    bc_copies = []
    for k, ref in enumerate((b_hbm, c_hbm)):
        copy = pltpu.make_async_remote_copy(
            src_ref=ref, dst_ref=bc.at[k, side], send_sem=bc_send.at[k], recv_sem=bc_recv.at[k],
            device_id={"head": mate}, device_id_type=MESH)
        copy.start()
        bc_copies.append(copy)
    i_copies = []
    for off in range(1, peers):
        copy = pltpu.make_async_remote_copy(
            src_ref=info.at[me], dst_ref=info.at[me], send_sem=i_send.at[off - 1], recv_sem=i_recv.at[off - 1],
            device_id={"ctx": (me + off) % peers}, device_id_type=MESH)
        copy.start()
        i_copies.append(copy)

    for off in range(1, peers):
        src = (me + peers - off) % peers
        pltpu.make_async_remote_copy(
            src_ref=info.at[src], dst_ref=info.at[src], send_sem=i_send.at[off - 1], recv_sem=i_recv.at[off - 1],
            device_id={"ctx": (me + off) % peers}, device_id_type=MESH).wait_recv()

    def seg_of(i):
        return info[(i + peers) % peers, 2:3, :]

    def prev_seg(i):
        return jnp.where(i == 0, -1.0, seg_of(i - 1))

    inputs[3].wait()
    start_mask = jnp.where(seg_col == prev_seg(me)[:, 0:128], 1.0, 0.0)
    for p in range(pairs):
        s = slice(p * 128, (p + 1) * 128)
        ws = jnp.exp(acx[:, s]) * start_mask
        ws_s[:, s] = ws
        hi, lo = split(d_ref[:, s].astype(F32) * ws)
        wdh[:, s] = hi
        wdl[:, s] = lo

    for copy in bc_copies:
        copy.wait_recv()
    inputs[5].wait()
    inputs[6].wait()
    b_full = jnp.concatenate([bc[0, 0], bc[0, 1]], axis=1)
    c_full = jnp.concatenate([bc[1, 0], bc[1, 1]], axis=1)
    b_t = b_full.T
    c_t = c_full.T
    def carry(i, k):
        return jnp.exp(info[i, pl.ds(k, 1), :]) * jnp.where(seg_of(i) == prev_seg(i), 1.0, 0.0)

    parts = fg.shape[0]
    cw = fg.shape[4]
    sib_carry = carry(sib, core)
    my_carry = carry(me, core)
    d_copies = []
    t_copies = []

    def forward(q):
        u = slice(q * cw, (q + 1) * cw)
        d_copies[2 * q].wait_recv()
        tbuf[q, core] = half[q] + sib_carry[:, u] * fg[q, core, core]
        d_copies[2 * q + 1].wait_recv()
        tbuf[q, 1 - core] = fg[q, 1 - core, core] + my_carry[:, u] * full[q, core]
        for off in range(1, chips):
            at = q * (chips - 1) + off - 1
            copy = pltpu.make_async_remote_copy(
                src_ref=tbuf.at[q, (chip + off) // chips], dst_ref=slots.at[at],
                send_sem=t_send.at[at], recv_sem=t_recv.at[at],
                device_id={"ctx": ((chip + off) % chips) * 2 + core}, device_id_type=MESH)
            copy.start()
            t_copies.append(copy)

    for q in range(parts):
        for k in range(2):
            s = slice(k * hw + q * cw, k * hw + (q + 1) * cw)
            fg[q, 0, k] = mm(b_t, wxh[:, s]) + mm(b_t, wxl[:, s])
            fg[q, 1, k] = mm(c_t, wdh[:, s]) + mm(c_t, wdl[:, s])
        half_copy = pltpu.make_async_remote_copy(
            src_ref=fg.at[q, 1 - core, 1 - core], dst_ref=half.at[q],
            send_sem=d_send.at[2 * q], recv_sem=d_recv.at[2 * q],
            device_id={"ctx": sib}, device_id_type=MESH)
        half_copy.start()
        full_copy = pltpu.make_async_remote_copy(
            src_ref=fg.at[q, core], dst_ref=full.at[q],
            send_sem=d_send.at[2 * q + 1], recv_sem=d_recv.at[2 * q + 1],
            device_id={"ctx": sib}, device_id_type=MESH)
        full_copy.start()
        d_copies += [half_copy, full_copy]
        if q:
            forward(q - 1)
    forward(parts - 1)


    bias[...] = jnp.where(
        (rows >= cols) & (jnp.concatenate([seg_col] * (tokens // 128), axis=1) == seg_row), 0.0, -1e30
    )
    inputs[4].wait()
    score_s[...] = mm(c_full, b_full, NT)
    dsc[...] = jnp.zeros_like(dsc)

    def pair_step(p, carried):
        s = pl.ds(pl.multiple_of(p * 128, 128), 128)
        x = x_ref[:, s]
        d = d_ref[:, s]
        gain = jnp.where(low, skip_ref[2 * p], skip_ref[2 * p + 1])
        out = gain * x.astype(F32)
        gx = gain * d.astype(F32)
        zero = jnp.zeros_like(x)
        total = dsc[...]
        for k in range(2):
            mine = low if k == 0 else jnp.logical_not(low)
            xm = jnp.where(mine, x, zero)
            dm = jnp.where(mine, d, zero)
            a_col = acx[:, s][:, k * head : k * head + 1]
            a_row = acum_s[pl.ds(2 * p + k, 1), :]
            table = jnp.exp((a_col - a_row) + bias[...])
            mixed = (table * score_s[...]).astype(BF)
            out = out + mm(mixed, xm)
            gx = gx + mm(mixed, dm, TN)
            total = total + mm(dm, x, NT) * table
        dsc[...] = total
        ssd_acc[:, s] = out
        gx_acc[:, s] = gx
        return carried

    lax.fori_loop(0, pairs, pair_step, 0)

    ds_hi, ds_lo = split(dsc[...])
    gb = mm(ds_hi, c_full, TN) + mm(ds_lo, c_full, TN)
    gc = mm(ds_hi, b_full) + mm(ds_lo, b_full)

    weights = []
    for off in range(1, chips):
        src = (chip + chips - off) % chips
        first = jnp.minimum(src, chip)
        final = jnp.maximum(src, chip)
        total = jnp.zeros((1, hw), F32)
        for i in range(peers):
            within = (i >= 2 * first + 2) & (i < 2 * final)
            total = total + jnp.where(within, info[i, pl.ds(core, 1), :], 0.0)
        weights.append(jnp.exp(total) * jnp.where(seg_of(2 * first + 1) == seg_of(2 * final - 1), 1.0, 0.0))
    sib_both = [carry(sib, k) for k in range(2)]

    def gather(q):
        u = slice(q * cw, (q + 1) * cw)
        st[q, core, 0] = jnp.zeros(st.shape[3:], F32)
        st[q, core, 1] = jnp.zeros(st.shape[3:], F32)
        for off in range(1, chips):
            later = 1 - (chip + chips - off) // chips
            at = q * (chips - 1) + off - 1
            t_copies[at].wait_recv()
            st[q, core, later] = st[q, core, later] + weights[off - 1][:, u] * slots[at]
        copy = pltpu.make_async_remote_copy(
            src_ref=st.at[q, core], dst_ref=st.at[q, core], send_sem=s_send.at[q], recv_sem=s_recv.at[q],
            device_id={"ctx": sib}, device_id_type=MESH)
        copy.start()
        return copy

    n = b_full.shape[1] // 2
    g_copies = []

    def send_off(which, grad):
        for k in range(2):
            gacc[k, which] = grad[:, k * n : (k + 1) * n]
        g_copy = pltpu.make_async_remote_copy(
            src_ref=gacc.at[1 - side, which], dst_ref=grecv.at[which],
            send_sem=g_send.at[which], recv_sem=g_recv.at[which],
            device_id={"head": mate}, device_id_type=MESH)
        g_copy.start()
        g_copies.append(g_copy)

    def absorb(q, copy, gb, gc):
        u = slice(q * cw, (q + 1) * cw)
        copy.wait_send()
        pltpu.make_async_remote_copy(
            src_ref=st.at[q, 1 - core], dst_ref=st.at[q, 1 - core], send_sem=s_send.at[q], recv_sem=s_recv.at[q],
            device_id={"ctx": sib}, device_id_type=MESH).wait_recv()
        for k in range(2):
            s = slice(k * hw + q * cw, k * hw + (q + 1) * cw)
            st[q, k, 1 - core] = sib_both[k][:, u] * st[q, k, 1 - core] + full[q, k]
            a_hi, a_lo = split(st[q, k, 1])
            gb = gb + mm(wxh[:, s], a_hi, NT) + mm(wxl[:, s], a_hi, NT) + mm(wxh[:, s], a_lo, NT)
        if q == parts - 1:
            send_off(0, gb)
        for k in range(2):
            s = slice(k * hw + q * cw, k * hw + (q + 1) * cw)
            s_hi, s_lo = split(st[q, k, 0])
            gc = gc + mm(wdh[:, s], s_hi, NT) + mm(wdl[:, s], s_hi, NT) + mm(wdh[:, s], s_lo, NT)
        if q == parts - 1:
            send_off(1, gc)
        return gb, gc

    def outputs(q):
        for k in range(2):
            s = slice(k * hw + q * cw, k * hw + (q + 1) * cw)
            s_hi, s_lo = split(st[q, k, 0])
            a_hi, a_lo = split(st[q, k, 1])
            ssd_ref[:, s] = (ssd_acc[:, s] + ws_s[:, s] * (mm(c_full, s_hi) + mm(c_full, s_lo))).astype(BF)
            gx_ref[:, s] = (gx_acc[:, s] + we_s[:, s] * (mm(b_full, a_hi) + mm(b_full, a_lo))).astype(BF)

    s_copy = gather(0)
    for q in range(parts):
        here = s_copy
        if q + 1 < parts:
            gb, gc = absorb(q, here, gb, gc)
            s_copy = gather(q + 1)
            outputs(q)
        else:
            gb, gc = absorb(q, here, gb, gc)
    outputs(parts - 1)

    g_copies[0].wait_recv()
    gb_ref[...] = (gacc[side, 0] + grecv[0]).astype(BF)
    g_copies[1].wait_recv()
    gc_ref[...] = (gacc[side, 1] + grecv[1]).astype(BF)

    for copy in bc_copies + i_copies + d_copies + t_copies + g_copies:
        copy.wait_send()


def per_device(peers, inputs, log_decay, in_b, in_c, seg_ids, skip_gain, grad_out):
    tokens, width = inputs.shape
    heads = log_decay.shape[0]
    cols = in_b.shape[1]
    n = 2 * cols
    hw = width // 2
    chips = peers // 2
    cw = hw // PARTS
    vm = pl.BlockSpec(memory_space=pltpu.VMEM)
    dma = pltpu.SemaphoreType.DMA
    results = pl.pallas_call(
        functools.partial(kernel, peers),
        out_shape=(
            jax.ShapeDtypeStruct((tokens, width), BF),
            jax.ShapeDtypeStruct((tokens, width), BF),
            jax.ShapeDtypeStruct((tokens, cols), BF),
            jax.ShapeDtypeStruct((tokens, cols), BF),
        ),
        in_specs=[pl.BlockSpec(memory_space=pltpu.HBM)] * 7,
        out_specs=(vm, vm, vm, vm),
        scratch_shapes=[
            pltpu.VMEM((tokens, width), BF),
            pltpu.VMEM((heads, tokens), F32),
            pltpu.VMEM((1, tokens), jnp.int32),
            pltpu.SMEM((heads,), F32),
            pltpu.VMEM((tokens, width), BF),
            dma((7,)),
            pltpu.VMEM((2, 2, tokens, cols), BF),
            pltpu.VMEM((peers, 4, hw), F32),
            pltpu.VMEM((heads, tokens), F32),
            pltpu.VMEM((tokens, width), F32),
            pltpu.VMEM((tokens, width), F32),
            pltpu.VMEM((tokens, width), F32),
            pltpu.VMEM((tokens, width), BF),
            pltpu.VMEM((tokens, width), BF),
            pltpu.VMEM((tokens, width), BF),
            pltpu.VMEM((tokens, width), BF),
            pltpu.VMEM((tokens, tokens), F32),
            pltpu.VMEM((tokens, tokens), F32),
            pltpu.VMEM((tokens, tokens), F32),
            pltpu.VMEM((tokens, width), F32),
            pltpu.VMEM((tokens, width), F32),
            pltpu.VMEM((PARTS, 2, 2, n, cw), F32),
            pltpu.VMEM((PARTS, 2, n, cw), F32),
            pltpu.VMEM((PARTS, n, cw), F32),
            pltpu.VMEM((PARTS, 2, n, cw), F32),
            pltpu.VMEM((PARTS * (chips - 1), n, cw), F32),
            pltpu.VMEM((PARTS, 2, 2, n, cw), F32),
            pltpu.VMEM((2, 2, tokens, cols), F32),
            pltpu.VMEM((2, tokens, cols), F32),
            dma((2,)),
            dma((2,)),
            dma((peers - 1,)),
            dma((peers - 1,)),
            dma((2 * PARTS,)),
            dma((2 * PARTS,)),
            dma((PARTS * (chips - 1),)),
            dma((PARTS * (chips - 1),)),
            dma((PARTS,)),
            dma((PARTS,)),
            dma((2,)),
            dma((2,)),
        ],
        compiler_params=pltpu.CompilerParams(
            collective_id=0, has_side_effects=True, vmem_limit_bytes=48 << 20
        ),
    )(*[pltpu.with_memory_space_constraint(a, pltpu.HBM) for a in (inputs, log_decay, in_b, in_c, seg_ids.reshape(1, tokens), skip_gain, grad_out)])
    hbm = pl.BlockSpec(memory_space=pltpu.HBM)
    return pl.pallas_call(
        hand_over,
        out_shape=tuple(jax.ShapeDtypeStruct(r.shape, r.dtype) for r in results),
        in_specs=[hbm] * 4,
        out_specs=(hbm,) * 4,
        scratch_shapes=[dma((4,))],
        compiler_params=pltpu.CompilerParams(vmem_limit_bytes=VMEM2),
    )(*results)


def hand_over(a, b, c, d, out_a, out_b, out_c, out_d, sem):
    copies = [
        pltpu.make_async_copy(src, dst, sem.at[k])
        for k, (src, dst) in enumerate(((a, out_a), (b, out_b), (c, out_c), (d, out_d)))
    ]
    for copy in copies:
        copy.start()
    for copy in copies:
        copy.wait()


def solution(mesh):
    return jax.shard_map(
        functools.partial(per_device, mesh.shape["ctx"]),
        mesh=mesh,
        in_specs=(
            P("ctx", "head"),
            P("head", "ctx"),
            P("ctx", "head"),
            P("ctx", "head"),
            P("ctx"),
            P("head"),
            P("ctx", "head"),
        ),
        out_specs=(P("ctx", "head"), P("ctx", "head"), P("ctx", "head"), P("ctx", "head")),
        check_vma=False,
    )
```
